256 devices in a mesh: brick: 8 (over x_lo, y), bulk: 32 (over x_hi, z, core).
Axes of the slice: x: 4 (x_hi: 2, x_lo: 2; x = x_hi * 2 + x_lo), y: 4, z: 8, core: 2. Of those that a mesh axis runs over, the one named last changes fastest.
Arguments:
- amp_traces: float32 [128, 2048, 256], P(None, ('bulk', 'brick')), may hold values from -6 to 6
- patch_owner: int32 [524288, 1], P(('brick', 'bulk')), may hold values from 0 to 31; in each aligned block of 2048 rows (0 to 2047, 2048 to 4095, ...) at most 256 rows name the same one
- patch_fault: int32 [524288], P(('brick', 'bulk')), may hold values from 0 to 15
- patch_trace: int32 [524288], P(('brick', 'bulk')), may hold values from 0 to 1023
- patch_offset: int32 [524288], P(('brick', 'bulk')), may hold values from 0 to 128
Outputs:
- fault_attr: float32 [128, 2048, 256], P('brick', 'bulk')
- fault_profile: float32 [4096, 128], P(('brick', 'bulk'))
The draws below stay inside these ranges and needn't reach their ends.
Inputs may be any that keep to these rules, and one draw needn't show every extreme that they name: `patch_owner`: among the 2048 patches of one device, at most 256 name the same owner, and in every draw some device has exactly 256 patches with one owner.
All inputs are finite; a program needn't handle non-finite values.
Results may differ from the reference program's by a relative error of at most 0.0003.
Values sent between devices are 32-bit elements; how exact they have to be, the bound alone decides.
A program may use at most 64 MiB of HBM per device.

```python
import math
import jax
import jax.numpy as jnp
import numpy as np
from jax import lax

CX = 16
CY = 64
NT = 256
PATCH = 128
P_DEV = 2048
F_DEV = 16
NX = 128
NY = 2048
CAP = 256
PATCHES = 524288
FAULTS = 4096
N_BRICK = 8
N_BULK = 32


def touch_ends(drawn, stream_key, low, top_value):
    dims = drawn.shape
    spot = [jax.random.randint(jax.random.fold_in(stream_key, axis), (), 0, dims[axis]) for axis in range(len(dims))]
    drawn = drawn.at[tuple(spot)].set(low)
    longest = dims.index(max(dims))
    spot[longest] = (spot[longest] + 1) % dims[longest]
    return drawn.at[tuple(spot)].set(top_value)


def block_levels(own_key, extent, split, low, high):
    loudness, own = 1.0, jax.random.fold_in(own_key, 6)
    for dim, parts in split:
        heights = jnp.exp(jax.random.uniform(jax.random.fold_in(own, dim), (parts,), jnp.float32, low / len(split), high / len(split)))
        loudness = loudness * jnp.repeat(heights, extent[dim] // parts).reshape([-1 if axis == dim else 1 for axis in range(len(extent))])
    return loudness


def deal_out(own_key, own, number, rows, amount, top, reach, lean):
    sequence = jax.random.permutation(own_key, amount)
    packed, ordinary = portions_of(amount, rows * top, reach, lean, True), portions_of(amount, rows * top, reach, lean, False)
    places = jnp.arange(amount)

    def named(tallies, rotation):
        used = int((tallies > 0).sum())
        fixed = max(1, used // 4)
        moved = fixed + (places - fixed + rotation * (used - fixed)) % max(1, amount - fixed)
        return jnp.zeros((amount,), jnp.int32).at[sequence[jnp.where(places < fixed, places, moved)]].set(jnp.asarray(tallies, jnp.int32))

    tallies = jnp.where(number % 4 == 0, named(packed, number // 4), named(ordinary, number - number // 4 - 1))
    mixed = jax.random.permutation(jax.random.fold_in(own, 3), amount)
    donor, sink = mixed[0:amount // 2 * 2:2], mixed[1:amount // 2 * 2:2]
    margin = jnp.minimum(tallies[donor] - 1, reach - tallies[sink]) // 2
    margin = jnp.where((donor == sequence[0]) | (sink == sequence[0]) | (tallies[sink] == 0), 0, jnp.maximum(margin, 0))
    moved = jax.random.randint(jax.random.fold_in(own, 4), (amount // 2,), 0, 1 << 20) % (margin + 1)
    tallies = tallies.at[donor].add(-moved).at[sink].add(moved)
    labels = jnp.searchsorted(jnp.cumsum(tallies), jnp.arange(rows * top), side="right").astype(jnp.int32)
    table = labels.reshape(top, rows).T
    table = table[jax.random.permutation(jax.random.fold_in(own, 1), rows)]
    rotation = jax.random.randint(jax.random.fold_in(own, 2), (rows, 1), 0, top)
    return jnp.take_along_axis(table, (jnp.arange(top)[None, :] + rotation) % top, axis=1)


def portions_of(count, total, bound, skew, full):
    loads = [(1 << 20) // math.isqrt(grade ** skew) + 1 for grade in range(1, count + 1)]
    largest = bound if full else min(bound, max(-(-total // count), total * loads[0] // sum(loads)))
    least = 1 if total - largest >= count - 1 else 0
    holding, rest = [largest] + [least] * (count - 1), total - largest - least * (count - 1)
    while rest > 0:
        movable = [i for i in range(1, count) if holding[i] < largest] or [i for i in range(1, count) if holding[i] < bound]
        whole, remaining = sum([loads[i] for i in movable]), rest
        for i in movable:
            addition = min(bound - holding[i], max(1, remaining * loads[i] // whole), rest)
            holding[i] = holding[i] + addition
            rest = rest - addition
    return np.array(holding)


def centred(rng, extent, spread, reach, cuts=(), held_as=jnp.bfloat16):
    drawn = jax.random.normal(rng, extent, jnp.float32) * spread
    if len(cuts) > 0:
        drawn = block_levels(rng, extent, cuts, -0.22, 0.18) * drawn
    return jnp.clip(drawn, min=-reach, max=reach).astype(held_as)


def setup_inputs(seed: int = 0) -> dict:
    keys = jax.random.split(jax.random.key(seed), 6)
    amp_traces = centred(keys[0], (NX, NY, NT), 1.0, 6.0, ((1, 256),), jnp.float32)
    patch_owner_keys = jax.random.split(jax.random.fold_in(keys[1], 1), PATCHES // P_DEV)
    patch_owner_turns = jax.random.permutation(jax.random.fold_in(keys[1], 3), PATCHES // P_DEV)
    patch_owner = jax.vmap(lambda own, number: deal_out(jax.random.fold_in(keys[1], 2), own, number, P_DEV, N_BULK, 1, CAP, 2))(patch_owner_keys, patch_owner_turns).reshape((PATCHES, 1))
    patch_fault = touch_ends(jax.random.randint(keys[2], (PATCHES,), 0, F_DEV), jax.random.fold_in(keys[2], 1), 0, F_DEV - 1).astype(jnp.int32)
    patch_trace = touch_ends(jax.random.randint(keys[3], (PATCHES,), 0, CX * CY), jax.random.fold_in(keys[3], 1), 0, (CX * CY) - 1).astype(jnp.int32)
    patch_offset = touch_ends(jax.random.randint(keys[4], (PATCHES,), 0, NT - PATCH + 1), jax.random.fold_in(keys[4], 1), 0, NT - PATCH).astype(jnp.int32)
    return dict(amp_traces=amp_traces, patch_owner=patch_owner, patch_fault=patch_fault, patch_trace=patch_trace, patch_offset=patch_offset)


def box_sum(values, radius, dimension):
    length = values.shape[dimension] - 2 * radius
    summed = lax.slice_in_dim(values, 0, length, axis=dimension)
    for offset in range(1, 2 * radius + 1):
        summed = summed + lax.slice_in_dim(values, offset, offset + length, axis=dimension)
    return summed


def time_sum(values, radius):
    widths = [(0, 0)] * (values.ndim - 1) + [(radius, radius)]
    return box_sum(jnp.pad(values, widths), radius, values.ndim - 1)


def gradient_energy(padded):
    slope_inline = 0.5 * (padded[2:, 1:-1, :] - padded[:-2, 1:-1, :])
    slope_cross = 0.5 * (padded[1:-1, 2:, :] - padded[1:-1, :-2, :])
    centre = jnp.pad(padded[1:-1, 1:-1, :], ((0, 0), (0, 0), (1, 1)))
    slope_time = 0.5 * (centre[:, :, 2:] - centre[:, :, :-2])
    return jnp.stack([slope_inline * slope_inline, slope_cross * slope_cross, slope_time * slope_time])


def smooth_tensor(energy):
    return time_sum(box_sum(box_sum(energy, 2, 1), 2, 2), 2)


def finish(tensor, near_amp):
    lateral = (tensor[0] + tensor[1]) / (tensor[0] + tensor[1] + tensor[2] + 1e-5)
    stack = box_sum(box_sum(near_amp, 1, 0), 1, 1)
    power = box_sum(box_sum(near_amp * near_amp, 1, 0), 1, 1)
    semblance = time_sum(stack * stack, 4) / (9.0 * time_sum(power, 4) + 1e-5)
    return (1.0 - semblance) * lateral


def reference(amp_traces, patch_owner, patch_fault, patch_trace, patch_offset):
    padded = jnp.pad(amp_traces, ((3, 3), (3, 3), (0, 0)))
    cross_pos = jnp.arange(NY + 4, dtype=jnp.int32) - 2
    cross_ok = ((cross_pos >= 0) & (cross_pos < NY)).astype(jnp.float32)

    def slab_attribute(index):
        slab = lax.dynamic_slice_in_dim(padded, (index * CX).astype(jnp.int32), CX + 6, 0)
        inline_pos = index * CX - 2 + jnp.arange(CX + 4, dtype=jnp.int32)
        inline_ok = ((inline_pos >= 0) & (inline_pos < NX)).astype(jnp.float32)
        weight_mask = inline_ok[:, None, None] * cross_ok[None, :, None]
        energy = gradient_energy(slab) * weight_mask[None]
        return finish(smooth_tensor(energy), slab[2:-2, 2:-2, :])

    slabs = lax.map(slab_attribute, jnp.arange(N_BRICK, dtype=jnp.int32))
    attribute = slabs.reshape(NX, NY, NT)
    patch_ids = jnp.arange(PATCHES, dtype=jnp.int32)
    device = patch_ids // P_DEV
    brick_of = device // N_BULK
    bulk_of = device % N_BULK
    inline_at = brick_of * CX + patch_trace // CY
    cross_at = bulk_of * CY + patch_trace % CY
    sample_index = patch_offset[:, None] + jnp.arange(PATCH, dtype=jnp.int32)[None, :]
    patch_rows = attribute[inline_at[:, None], cross_at[:, None], sample_index]
    fault_ids = brick_of * (F_DEV * N_BULK) + patch_owner[:, 0] * F_DEV + patch_fault
    summed = jax.ops.segment_sum(patch_rows, fault_ids, num_segments=FAULTS)
    counts = jax.ops.segment_sum(jnp.ones((PATCHES,), jnp.float32), fault_ids, num_segments=FAULTS)
    profile = summed / jnp.maximum(counts, 1.0)[:, None]
    return attribute, profile
```

```python
import functools

import jax
import jax.numpy as jnp
from jax import lax
from jax.experimental import pallas as pl
from jax.experimental.pallas import tpu as pltpu
from jax.sharding import PartitionSpec as P

MESH = pl.DeviceIdType.MESH
F32, BF16 = jnp.float32, jnp.bfloat16
NB, NK = 8, 32
CX, CY, NT, HALF = 16, 64, 256, 128
PATCHES, PATCH, F_DEV = 2048, 128, 16
FAULTS = NK * F_DEV
TRACES = CX * CY
GROUP = 4
GROUPS = CX // GROUP
PIECES = ((0, 10), (10, 4), (14, 4), (18, 4))
FIRST_ROWS = 7
LAST_ROWS = 1
Q = 72
NEAR_C = 80


def split(x):
    hi = x.astype(BF16)
    return hi, (x - hi.astype(F32)).astype(BF16)


def kernel(amp, owner, fault, trace, offset, attr_out, prof_out,
           near, ep, eq, vp, vq, w1, w2, f5, f9, t5, t9, b5, b9, attr_v, attr_bf,
           pick, offs, seg, rows, part, rbuf, cnts, cbuf,
           self_sem, send_sem, recv_sem, hsend_sem, hrecv_sem, out_sem,
           psend_sem, precv_sem, csend_sem, crecv_sem):
    b, k = lax.axis_index("brick"), lax.axis_index("bulk")

    barrier = pltpu.get_barrier_semaphore()
    for d in range(1, NB):
        pl.semaphore_signal(barrier, inc=1, device_id=(lax.rem(b + d, NB), k), device_id_type=MESH)
    for d in range(1, NK):
        pl.semaphore_signal(barrier, inc=1, device_id=(b, lax.rem(k + d, NK)), device_id_type=MESH)

    def for_variant(g, t, act):
        start, count = PIECES[g]
        if g == 0:
            @pl.when(t == 0)
            def _():
                act(count - FIRST_ROWS, FIRST_ROWS)

            @pl.when(t != 0)
            def _():
                act(start, count)
        elif g == GROUPS - 1:
            @pl.when(t == NB - 1)
            def _():
                act(start, LAST_ROWS)

            @pl.when(t != NB - 1)
            def _():
                act(start, count)
        else:
            act(start, count)

    def strip(ref, start, count, s):
        return ref.at[pl.ds(start, count), :, pl.ds(pl.multiple_of(8 + 8 * s, 8), 8), :]

    def block(t, start, count):
        return amp.at[pl.ds(t * CX - 3 + start, count)]

    def self_copy(g, act):
        def go(start, count):
            act(pltpu.make_async_copy(block(b, start, count), strip(near, start, count, b), self_sem.at[g]))
        for_variant(g, b, go)

    for g in range(GROUPS):
        self_copy(g, lambda copy: copy.start())

    @pl.when(b == 0)
    def _():
        near[0:3] = jnp.zeros((3, 2, NEAR_C, HALF), F32)

    @pl.when(b == NB - 1)
    def _():
        near[19:22] = jnp.zeros((3, 2, NEAR_C, HALF), F32)

    @pl.when(k == 0)
    def _():
        near[:, :, 0:8, :] = jnp.zeros((22, 2, 8, HALF), F32)

    @pl.when(k == NK - 1)
    def _():
        near[:, :, 72:80, :] = jnp.zeros((22, 2, 8, HALF), F32)

    pl.semaphore_wait(barrier, NB - 1 + NK - 1)

    peers = [(0, 1), (1, 0), (0, 3), (1, 1), (0, 2), (1, 3), (1, 2)]

    def peer(dx, dy):
        return lax.rem(b // 4 + dx, 2) * 4 + lax.rem(lax.rem(b, 4) + dy, 4)

    def send(g, t, act):
        def go(start, count):
            act(pltpu.make_async_remote_copy(
                src_ref=block(t, start, count), dst_ref=strip(near, start, count, b),
                send_sem=send_sem.at[g, t], recv_sem=recv_sem.at[g, b],
                device_id=(t, k), device_id_type=MESH))
        for_variant(g, t, go)

    def arrived(g, s):
        def go(start, count):
            pltpu.make_async_remote_copy(
                src_ref=block(b, start, count), dst_ref=strip(near, start, count, s),
                send_sem=send_sem.at[g, s], recv_sem=recv_sem.at[g, s],
                device_id=(s, k), device_id_type=MESH).wait_recv()
        for_variant(g, b, go)

    for g in range(GROUPS):
        for dx, dy in peers:
            send(g, peer(dx, dy), lambda copy: copy.start())

    def halo_up(g, act):
        def go(start, count):
            act(pltpu.make_async_remote_copy(
                src_ref=near.at[pl.ds(start, count), :, 64:72, :],
                dst_ref=near.at[pl.ds(start, count), :, 0:8, :],
                send_sem=hsend_sem.at[g, 0], recv_sem=hrecv_sem.at[g, 0],
                device_id=(b, lax.rem(k + 1, NK)), device_id_type=MESH))
        for_variant(g, b, go)

    def halo_down(g, act):
        def go(start, count):
            act(pltpu.make_async_remote_copy(
                src_ref=near.at[pl.ds(start, count), :, 8:16, :],
                dst_ref=near.at[pl.ds(start, count), :, 72:80, :],
                send_sem=hsend_sem.at[g, 1], recv_sem=hrecv_sem.at[g, 1],
                device_id=(b, lax.rem(k + NK - 1, NK)), device_id_type=MESH))
        for_variant(g, b, go)

    row = lax.broadcasted_iota(jnp.int32, (NT, NT), 0)
    col = lax.broadcasted_iota(jnp.int32, (NT, NT), 1)
    near_diag = jnp.abs(row - col)
    for half in range(2):
        b5[half * NT:(half + 1) * NT] = jnp.where(near_diag <= 2, 1.0, 0.0).astype(BF16)
        b9[half * NT:(half + 1) * NT] = jnp.where(near_diag <= 4, 1.0, 0.0).astype(BF16)

    lane = lax.broadcasted_iota(jnp.int32, (HALF, HALF), 1)
    sub = lax.broadcasted_iota(jnp.int32, (HALF, HALF), 0)

    @pl.loop(0, PATCHES // HALF)
    def _(m):
        at = pl.ds(pl.multiple_of(m * HALF, HALF), HALF)
        traces = jnp.broadcast_to(trace[pl.ds(m, 1), :], (HALF, HALF)).T
        for j in range(TRACES // HALF):
            pick[at, j * HALF:(j + 1) * HALF] = jnp.where(traces == lane + j * HALF, 1.0, 0.0).astype(BF16)
        offs[at, :] = jnp.broadcast_to(offset[pl.ds(m, 1), :], (HALF, HALF)).T + lane
        label = jnp.broadcast_to(owner[pl.ds(m, 1), :] * F_DEV + fault[pl.ds(m, 1), :], (HALF, HALF))
        for j in range(FAULTS // HALF):
            seg[j * HALF:(j + 1) * HALF, at] = jnp.where(label == sub + j * HALF, 1.0, 0.0).astype(BF16)

    def count_body(m, total):
        own = jnp.broadcast_to(owner[pl.ds(m, 1), :], (NK, HALF)) == sub[:NK]
        of = jnp.broadcast_to(fault[pl.ds(m, 1), :], (HALF, HALF)) == sub
        return total + lax.dot_general(
            jnp.where(own, 1.0, 0.0).astype(BF16), jnp.where(of, 1.0, 0.0).astype(BF16),
            (((1,), (1,)), ((), ())), preferred_element_type=F32)

    cnts[...] = lax.fori_loop(0, PATCHES // HALF, count_body, jnp.zeros((NK, HALF), F32))

    def count_send(d):
        to = lax.rem(k + d, NK)
        return pltpu.make_async_remote_copy(
            src_ref=cnts.at[pl.ds(to, 1)], dst_ref=cbuf.at[pl.ds(k, 1)],
            send_sem=csend_sem.at[to], recv_sem=crecv_sem.at[k],
            device_id=(b, to), device_id_type=MESH)

    @pl.loop(1, NK)
    def _(d):
        count_send(d).start()

    lanes = lax.broadcasted_iota(jnp.int32, (Q, HALF), 1)

    def energy_row(e):
        low, high = near[e + 1, 0, 6:78, :], near[e + 1, 1, 6:78, :]
        low_r, high_r = pltpu.roll(low, 1, 1), pltpu.roll(high, 1, 1)
        low_l, high_l = pltpu.roll(low, HALF - 1, 1), pltpu.roll(high, HALF - 1, 1)
        first, last = lanes == 0, lanes == HALF - 1
        dt = (
            jnp.where(last, high_l, low_l) - jnp.where(first, 0.0, low_r),
            jnp.where(last, 0.0, high_l) - jnp.where(first, low_r, high_r),
        )
        for h in range(2):
            dx = near[e + 2, h, 6:78, :] - near[e, h, 6:78, :]
            dy = near[e + 1, h, 7:79, :] - near[e + 1, h, 5:77, :]
            lateral = dx * dx + dy * dy
            ep[e, h] = lateral
            eq[e, h] = lateral + dt[h] * dt[h]

    def fields_row(i):
        slot = lax.rem(i, GROUP) * 2
        for h in range(2):
            vp[h] = ep[i, h] + ep[i + 1, h] + ep[i + 2, h] + ep[i + 3, h] + ep[i + 4, h]
            vq[h] = eq[i, h] + eq[i + 1, h] + eq[i + 2, h] + eq[i + 3, h] + eq[i + 4, h]
            a, c, d = near[i + 2, h, 7:79, :], near[i + 3, h, 7:79, :], near[i + 4, h, 7:79, :]
            w1[h] = a + c + d
            w2[h] = a * a + c * c + d * d
        for h in range(2):
            box = [sum(v[h, o:o + CY, :] for o in range(5)) for v in (vp, vq)]
            stack, power = (sum(w[h, o:o + CY, :] for o in range(3)) for w in (w1, w2))
            for target, values in ((f5, box), (f9, [9.0 * power - stack * stack, power])):
                for n in range(2):
                    hi, lo = split(values[n])
                    at = pl.ds(pl.multiple_of((slot + n) * CY, CY), CY)
                    target[at, h * HALF:(h + 1) * HALF] = hi
                    target[at, NT + h * HALF:NT + (h + 1) * HALF] = lo

    def finish_row(i):
        slot = lax.rem(i, GROUP) * 2
        top, low = (pl.ds(pl.multiple_of((slot + n) * CY, CY), CY) for n in range(2))
        value = ((t9[top, :] + 1e-05) * t5[top, :]) / ((9.0 * t9[low, :] + 1e-05) * (t5[low, :] + 4e-05))
        attr_v[i] = value
        hi, lo = split(value)
        at = pl.ds(pl.multiple_of(i * CY, CY), CY)
        attr_bf[at, 0:NT] = hi
        attr_bf[at, NT:2 * NT] = lo

    def out_copy(g):
        at = slice(g * GROUP, (g + 1) * GROUP)
        return pltpu.make_async_copy(attr_v.at[at], attr_out.at[at], out_sem.at[g])

    for g in range(GROUPS):
        self_copy(g, lambda copy: copy.wait())
        for dx, dy in peers:
            arrived(g, peer(dx, dy))

        @pl.when(k != NK - 1)
        def _():
            halo_up(g, lambda copy: copy.start())

        @pl.when(k != 0)
        def _():
            halo_down(g, lambda copy: copy.start())

        @pl.when(k != 0)
        def _():
            halo_up(g, lambda copy: copy.wait_recv())

        @pl.when(k != NK - 1)
        def _():
            halo_down(g, lambda copy: copy.wait_recv())

        e0, e1 = (0, 8) if g == 0 else (4 * g + 4, 4 * g + 8)
        pl.loop(e0, e1)(energy_row)

        @pl.when(k == 0)
        def _():
            ep[e0:e1, :, 0:2, :] = jnp.zeros((e1 - e0, 2, 2, HALF), F32)
            eq[e0:e1, :, 0:2, :] = jnp.zeros((e1 - e0, 2, 2, HALF), F32)

        @pl.when(k == NK - 1)
        def _():
            ep[e0:e1, :, 66:68, :] = jnp.zeros((e1 - e0, 2, 2, HALF), F32)
            eq[e0:e1, :, 66:68, :] = jnp.zeros((e1 - e0, 2, 2, HALF), F32)

        if g in (0, GROUPS - 1):
            edge = 0 if g == 0 else 18

            @pl.when(b == (0 if g == 0 else NB - 1))
            def _():
                ep[edge:edge + 2] = jnp.zeros((2, 2, Q, HALF), F32)
                eq[edge:edge + 2] = jnp.zeros((2, 2, Q, HALF), F32)

        pl.loop(g * GROUP, (g + 1) * GROUP)(fields_row)
        t5[...] = jnp.dot(f5[...], b5[...], preferred_element_type=F32)
        t9[...] = jnp.dot(f9[...], b9[...], preferred_element_type=F32)
        pl.loop(g * GROUP, (g + 1) * GROUP)(finish_row)
        out_copy(g).start()

    chunk = 256

    @pl.loop(0, PATCHES // chunk)
    def _(m):
        at = pl.ds(pl.multiple_of(m * chunk, chunk), chunk)
        picked = jnp.dot(pick[at, :], attr_bf[...], preferred_element_type=F32)
        early = picked[:, 0:HALF] + picked[:, NT:NT + HALF]
        late = picked[:, HALF:NT] + picked[:, NT + HALF:2 * NT]
        index = offs[at, :]
        turn = jnp.bitwise_and(index, HALF - 1)
        taken = jnp.where(
            index < HALF,
            jnp.take_along_axis(early, turn, axis=1, mode="promise_in_bounds"),
            jnp.take_along_axis(late, turn, axis=1, mode="promise_in_bounds"))
        hi, lo = split(taken)
        rows[at, 0:HALF] = hi
        rows[at, HALF:2 * HALF] = lo

    both = jnp.dot(seg[...], rows[...], preferred_element_type=F32)
    part[...] = both[:, 0:HALF] + both[:, HALF:2 * HALF]

    def part_send(d):
        to = lax.rem(k + d, NK)
        return pltpu.make_async_remote_copy(
            src_ref=part.at[pl.ds(pl.multiple_of(to * F_DEV, F_DEV), F_DEV)], dst_ref=rbuf.at[k],
            send_sem=psend_sem.at[to], recv_sem=precv_sem.at[k],
            device_id=(b, to), device_id_type=MESH)

    def part_recv(d):
        source = lax.rem(k + NK - d, NK)
        return pltpu.make_async_remote_copy(
            src_ref=part.at[0:F_DEV], dst_ref=rbuf.at[source],
            send_sem=psend_sem.at[source], recv_sem=precv_sem.at[source],
            device_id=(b, source), device_id_type=MESH)

    def count_recv(d):
        source = lax.rem(k + NK - d, NK)
        return pltpu.make_async_remote_copy(
            src_ref=cnts.at[0:1], dst_ref=cbuf.at[pl.ds(source, 1)],
            send_sem=csend_sem.at[source], recv_sem=crecv_sem.at[source],
            device_id=(b, source), device_id_type=MESH)

    @pl.loop(1, NK)
    def _(d):
        part_send(d).start()

    def count_sum(d, total):
        count_recv(d).wait_recv()
        return total + cbuf[pl.ds(lax.rem(k + NK - d, NK), 1), :]

    number = lax.fori_loop(1, NK, count_sum, cnts[pl.ds(k, 1), :])
    column = jnp.sum(
        jnp.where(lane[:F_DEV] == sub[:F_DEV], jnp.broadcast_to(number, (F_DEV, HALF)), 0.0),
        axis=1, keepdims=True)

    def part_sum(d, total):
        part_recv(d).wait_recv()
        return total + rbuf[lax.rem(k + NK - d, NK)]

    own_part = part[pl.ds(pl.multiple_of(k * F_DEV, F_DEV), F_DEV), :]
    summed = lax.fori_loop(1, NK, part_sum, own_part)
    prof_out[...] = summed / jnp.maximum(column, 1.0)

    for g in range(GROUPS):
        out_copy(g).wait()
        for dx, dy in peers:
            send(g, peer(dx, dy), lambda copy: copy.wait_send())

        @pl.when(k != NK - 1)
        def _():
            halo_up(g, lambda copy: copy.wait_send())

        @pl.when(k != 0)
        def _():
            halo_down(g, lambda copy: copy.wait_send())

    @pl.loop(1, NK)
    def _(d):
        count_send(d).wait_send()
        part_send(d).wait_send()


def local(amp_traces, patch_owner, patch_fault, patch_trace, patch_offset):
    halves = amp_traces.reshape(NB * CX, 8, 2, HALF).transpose(0, 2, 1, 3)
    table = (PATCHES // HALF, HALF)
    vmem = pl.BlockSpec(memory_space=pltpu.VMEM)
    dma = pltpu.SemaphoreType.DMA
    return pl.pallas_call(
        kernel,
        out_shape=(
            jax.ShapeDtypeStruct((CX, CY, NT), F32),
            jax.ShapeDtypeStruct((F_DEV, PATCH), F32),
        ),
        in_specs=[pl.BlockSpec(memory_space=pl.ANY)] + [vmem] * 4,
        out_specs=(pl.BlockSpec(memory_space=pl.ANY), vmem),
        scratch_shapes=[
            pltpu.VMEM((CX + 6, 2, NEAR_C, HALF), F32),
            pltpu.VMEM((CX + 4, 2, Q, HALF), F32),
            pltpu.VMEM((CX + 4, 2, Q, HALF), F32),
            pltpu.VMEM((2, Q, HALF), F32),
            pltpu.VMEM((2, Q, HALF), F32),
            pltpu.VMEM((2, Q, HALF), F32),
            pltpu.VMEM((2, Q, HALF), F32),
            pltpu.VMEM((GROUP * 2 * CY, 2 * NT), BF16),
            pltpu.VMEM((GROUP * 2 * CY, 2 * NT), BF16),
            pltpu.VMEM((GROUP * 2 * CY, NT), F32),
            pltpu.VMEM((GROUP * 2 * CY, NT), F32),
            pltpu.VMEM((2 * NT, NT), BF16),
            pltpu.VMEM((2 * NT, NT), BF16),
            pltpu.VMEM((CX, CY, NT), F32),
            pltpu.VMEM((TRACES, 2 * NT), BF16),
            pltpu.VMEM((PATCHES, TRACES), BF16),
            pltpu.VMEM((PATCHES, HALF), jnp.int32),
            pltpu.VMEM((FAULTS, PATCHES), BF16),
            pltpu.VMEM((PATCHES, 2 * HALF), BF16),
            pltpu.VMEM((FAULTS, PATCH), F32),
            pltpu.VMEM((NK, F_DEV, PATCH), F32),
            pltpu.VMEM((NK, HALF), F32),
            pltpu.VMEM((NK, HALF), F32),
            dma((GROUPS,)),
            dma((GROUPS, NB)),
            dma((GROUPS, NB)),
            dma((GROUPS, 2)),
            dma((GROUPS, 2)),
            dma((GROUPS,)),
            dma((NK,)),
            dma((NK,)),
            dma((NK,)),
            dma((NK,)),
        ],
        compiler_params=pltpu.CompilerParams(collective_id=0, has_side_effects=True),
        name="fault_attribute",
    )(
        halves,
        patch_owner.reshape(table),
        patch_fault.reshape(table),
        patch_trace.reshape(table),
        patch_offset.reshape(table),
    )


def solution(mesh):
    in_specs = (
        P(None, ("bulk", "brick"), None),
        P(("brick", "bulk"), None),
        P(("brick", "bulk")),
        P(("brick", "bulk")),
        P(("brick", "bulk")),
    )
    out_specs = (P("brick", "bulk", None), P(("brick", "bulk"), None))
    return jax.shard_map(local, mesh=mesh, in_specs=in_specs, out_specs=out_specs, check_vma=False)
```

```python
import functools

import jax
import jax.numpy as jnp
from jax import lax
from jax.experimental import pallas as pl
from jax.experimental.pallas import tpu as pltpu
from jax.sharding import PartitionSpec as P

MESH = pl.DeviceIdType.MESH
F32, BF16 = jnp.float32, jnp.bfloat16
NB, NK = 8, 32
CX, CY, NT, HALF = 16, 64, 256, 128
PATCHES, PATCH, F_DEV = 2048, 128, 16
FAULTS = NK * F_DEV
TRACES = CX * CY
GROUP = 4
GROUPS = CX // GROUP
PIECES = ((0, 10), (10, 4), (14, 4), (18, 4))
FIRST_ROWS = 7
LAST_ROWS = 1
Q = 72
NEAR_C = 80


def split(x):
    hi = x.astype(BF16)
    return hi, (x - hi.astype(F32)).astype(BF16)


def kernel(amp, owner_in, fault_in, trace_in, offset_in, attr_out, prof_out,
           owner, fault, trace, offset, near, ep, eq, vp, vq, w1, w2, f5, f9, t5, t9, b5, b9, attr_bf, picked,
           pick, offs, seg, rows, part, rbuf, cnts, cbuf,
           index_sem, self_sem, send_sem, recv_sem, hsend_sem, hrecv_sem,
           psend_sem, precv_sem, csend_sem, crecv_sem):
    b, k = lax.axis_index("brick"), lax.axis_index("bulk")

    barrier = pltpu.get_barrier_semaphore()
    for d in range(1, NB):
        pl.semaphore_signal(barrier, inc=1, device_id=(lax.rem(b + d, NB), k), device_id_type=MESH)
    for d in range(1, NK):
        pl.semaphore_signal(barrier, inc=1, device_id=(b, lax.rem(k + d, NK)), device_id_type=MESH)

    tables = [
        pltpu.make_async_copy(source, target, index_sem.at[n])
        for n, (source, target) in enumerate(
            ((owner_in, owner), (fault_in, fault), (trace_in, trace), (offset_in, offset)))
    ]
    for copy in tables:
        copy.start()

    def for_variant(g, t, act):
        start, count = PIECES[g]
        if g == 0:
            @pl.when(t == 0)
            def _():
                act(count - FIRST_ROWS, FIRST_ROWS)

            @pl.when(t != 0)
            def _():
                act(start, count)
        elif g == GROUPS - 1:
            @pl.when(t == NB - 1)
            def _():
                act(start, LAST_ROWS)

            @pl.when(t != NB - 1)
            def _():
                act(start, count)
        else:
            act(start, count)

    def strip(ref, start, count, s):
        return ref.at[pl.ds(start, count), :, pl.ds(pl.multiple_of(8 + 8 * s, 8), 8), :]

    def block(t, start, count):
        return amp.at[pl.ds(t * CX - 3 + start, count)]

    def self_copy(g, act):
        def go(start, count):
            act(pltpu.make_async_copy(block(b, start, count), strip(near, start, count, b), self_sem.at[g]))
        for_variant(g, b, go)

    for g in range(GROUPS):
        self_copy(g, lambda copy: copy.start())

    @pl.when(b == 0)
    def _():
        near[0:3] = jnp.zeros((3, 2, NEAR_C, HALF), F32)

    @pl.when(b == NB - 1)
    def _():
        near[19:22] = jnp.zeros((3, 2, NEAR_C, HALF), F32)

    @pl.when(k == 0)
    def _():
        near[:, :, 0:8, :] = jnp.zeros((22, 2, 8, HALF), F32)

    @pl.when(k == NK - 1)
    def _():
        near[:, :, 72:80, :] = jnp.zeros((22, 2, 8, HALF), F32)

    pl.semaphore_wait(barrier, NB - 1 + NK - 1)

    peers = [(0, 1), (1, 0), (0, 3), (1, 1), (0, 2), (1, 3), (1, 2)]

    def peer(dx, dy):
        return lax.rem(b // 4 + dx, 2) * 4 + lax.rem(lax.rem(b, 4) + dy, 4)

    def send(g, t, act):
        def go(start, count):
            act(pltpu.make_async_remote_copy(
                src_ref=block(t, start, count), dst_ref=strip(near, start, count, b),
                send_sem=send_sem.at[g, t], recv_sem=recv_sem.at[g, b],
                device_id=(t, k), device_id_type=MESH))
        for_variant(g, t, go)

    def arrived(g, s):
        def go(start, count):
            pltpu.make_async_remote_copy(
                src_ref=block(b, start, count), dst_ref=strip(near, start, count, s),
                send_sem=send_sem.at[g, s], recv_sem=recv_sem.at[g, s],
                device_id=(s, k), device_id_type=MESH).wait_recv()
        for_variant(g, b, go)

    def send_piece(g):
        for dx, dy in peers:
            send(g, peer(dx, dy), lambda copy: copy.start())

    send_piece(0)
    send_piece(1)

    def halo_up(g, act):
        def go(start, count):
            act(pltpu.make_async_remote_copy(
                src_ref=near.at[pl.ds(start, count), :, 64:72, :],
                dst_ref=near.at[pl.ds(start, count), :, 0:8, :],
                send_sem=hsend_sem.at[g, 0], recv_sem=hrecv_sem.at[g, 0],
                device_id=(b, lax.rem(k + 1, NK)), device_id_type=MESH))
        for_variant(g, b, go)

    def halo_down(g, act):
        def go(start, count):
            act(pltpu.make_async_remote_copy(
                src_ref=near.at[pl.ds(start, count), :, 8:16, :],
                dst_ref=near.at[pl.ds(start, count), :, 72:80, :],
                send_sem=hsend_sem.at[g, 1], recv_sem=hrecv_sem.at[g, 1],
                device_id=(b, lax.rem(k + NK - 1, NK)), device_id_type=MESH))
        for_variant(g, b, go)

    row = lax.broadcasted_iota(jnp.int32, (NT, NT), 0)
    col = lax.broadcasted_iota(jnp.int32, (NT, NT), 1)
    near_diag = jnp.abs(row - col)
    for half in range(2):
        b5[half * NT:(half + 1) * NT] = jnp.where(near_diag <= 2, 1.0, 0.0).astype(BF16)
        b9[half * NT:(half + 1) * NT] = jnp.where(near_diag <= 4, 1.0, 0.0).astype(BF16)

    lane = lax.broadcasted_iota(jnp.int32, (HALF, HALF), 1)
    sub = lax.broadcasted_iota(jnp.int32, (HALF, HALF), 0)

    for copy in tables:
        copy.wait()

    @pl.loop(0, PATCHES // HALF)
    def _(m):
        at = pl.ds(pl.multiple_of(m * HALF, HALF), HALF)
        traces = jnp.broadcast_to(trace[pl.ds(m, 1), :], (HALF, HALF)).T
        for j in range(TRACES // HALF):
            pick[at, j * HALF:(j + 1) * HALF] = jnp.where(traces == lane + j * HALF, 1.0, 0.0).astype(BF16)
        offs[at, :] = jnp.broadcast_to(offset[pl.ds(m, 1), :], (HALF, HALF)).T + lane
        label = jnp.broadcast_to(owner[pl.ds(m, 1), :] * F_DEV + fault[pl.ds(m, 1), :], (HALF, HALF))
        for j in range(FAULTS // HALF):
            seg[j * HALF:(j + 1) * HALF, at] = jnp.where(label == sub + j * HALF, 1.0, 0.0).astype(BF16)

    def count_body(m, total):
        own = jnp.broadcast_to(owner[pl.ds(m, 1), :], (NK, HALF)) == sub[:NK]
        of = jnp.broadcast_to(fault[pl.ds(m, 1), :], (HALF, HALF)) == sub
        return total + lax.dot_general(
            jnp.where(own, 1.0, 0.0).astype(BF16), jnp.where(of, 1.0, 0.0).astype(BF16),
            (((1,), (1,)), ((), ())), preferred_element_type=F32)

    cnts[...] = lax.fori_loop(0, PATCHES // HALF, count_body, jnp.zeros((NK, HALF), F32))

    def count_send(d):
        to = lax.rem(k + d, NK)
        return pltpu.make_async_remote_copy(
            src_ref=cnts.at[pl.ds(to, 1)], dst_ref=cbuf.at[pl.ds(k, 1)],
            send_sem=csend_sem.at[to], recv_sem=crecv_sem.at[k],
            device_id=(b, to), device_id_type=MESH)

    @pl.loop(1, NK)
    def _(d):
        count_send(d).start()

    lanes = lax.broadcasted_iota(jnp.int32, (Q, HALF), 1)

    def energy_row(e):
        low, high = near[e + 1, 0, 6:78, :], near[e + 1, 1, 6:78, :]
        low_r, high_r = pltpu.roll(low, 1, 1), pltpu.roll(high, 1, 1)
        low_l, high_l = pltpu.roll(low, HALF - 1, 1), pltpu.roll(high, HALF - 1, 1)
        first, last = lanes == 0, lanes == HALF - 1
        dt = (
            jnp.where(last, high_l, low_l) - jnp.where(first, 0.0, low_r),
            jnp.where(last, 0.0, high_l) - jnp.where(first, low_r, high_r),
        )
        for h in range(2):
            dx = near[e + 2, h, 6:78, :] - near[e, h, 6:78, :]
            dy = near[e + 1, h, 7:79, :] - near[e + 1, h, 5:77, :]
            lateral = dx * dx + dy * dy
            ep[e, h] = lateral
            eq[e, h] = lateral + dt[h] * dt[h]

    def fields_row(i):
        slot = lax.rem(i, GROUP) * 2
        for h in range(2):
            vp[h] = ep[i, h] + ep[i + 1, h] + ep[i + 2, h] + ep[i + 3, h] + ep[i + 4, h]
            vq[h] = eq[i, h] + eq[i + 1, h] + eq[i + 2, h] + eq[i + 3, h] + eq[i + 4, h]
            a, c, d = near[i + 2, h, 7:79, :], near[i + 3, h, 7:79, :], near[i + 4, h, 7:79, :]
            w1[h] = a + c + d
            w2[h] = a * a + c * c + d * d
        for h in range(2):
            box = [sum(v[h, o:o + CY, :] for o in range(5)) for v in (vp, vq)]
            stack, power = (sum(w[h, o:o + CY, :] for o in range(3)) for w in (w1, w2))
            for target, values in ((f5, box), (f9, [9.0 * power - stack * stack, power])):
                for n in range(2):
                    hi, lo = split(values[n])
                    at = pl.ds(pl.multiple_of((slot + n) * CY, CY), CY)
                    target[at, h * HALF:(h + 1) * HALF] = hi
                    target[at, NT + h * HALF:NT + (h + 1) * HALF] = lo

    def finish_row(i):
        slot = lax.rem(i, GROUP) * 2
        top, low = (pl.ds(pl.multiple_of((slot + n) * CY, CY), CY) for n in range(2))
        value = ((t9[top, :] + 1e-05) * t5[top, :]) / ((9.0 * t9[low, :] + 1e-05) * (t5[low, :] + 4e-05))
        attr_out[i] = value
        hi, lo = split(value)
        at = lax.rem(i, GROUP) * CY
        attr_bf[pl.ds(pl.multiple_of(at, CY), CY), :] = hi
        attr_bf[pl.ds(pl.multiple_of(GROUP * CY + at, CY), CY), :] = lo

    chunk = 512

    def pick_traces(g):
        @pl.loop(0, PATCHES // chunk)
        def _(m):
            at = pl.ds(pl.multiple_of(m * chunk, chunk), chunk)
            chosen = pick[at, g * GROUP * CY:(g + 1) * GROUP * CY]
            found = jnp.dot(jnp.concatenate([chosen, chosen], axis=1), attr_bf[...], preferred_element_type=F32)
            if g > 0:
                found = found + picked[at, :]
            if g < GROUPS - 1:
                picked[at, :] = found
                return
            early, late = found[:, :HALF], found[:, HALF:]
            index = offs[at, :]
            turn = jnp.bitwise_and(index, HALF - 1)
            taken = jnp.where(
                index < HALF,
                jnp.take_along_axis(early, turn, axis=1, mode="promise_in_bounds"),
                jnp.take_along_axis(late, turn, axis=1, mode="promise_in_bounds"))
            hi, lo = split(taken)
            rows[at, 0:HALF] = hi
            rows[at, HALF:2 * HALF] = lo

    def arrive(g):
        self_copy(g, lambda copy: copy.wait())
        for dx, dy in peers:
            arrived(g, peer(dx, dy))

        @pl.when(k != NK - 1)
        def _():
            halo_up(g, lambda copy: copy.start())

        @pl.when(k != 0)
        def _():
            halo_down(g, lambda copy: copy.start())

        if g + 2 < GROUPS:
            send_piece(g + 2)

    def compute(g):
        @pl.when(k != 0)
        def _():
            halo_up(g, lambda copy: copy.wait_recv())

        @pl.when(k != NK - 1)
        def _():
            halo_down(g, lambda copy: copy.wait_recv())

        e0, e1 = (0, 8) if g == 0 else (4 * g + 4, 4 * g + 8)
        pl.loop(e0, e1)(energy_row)

        @pl.when(k == 0)
        def _():
            ep[e0:e1, :, 0:2, :] = jnp.zeros((e1 - e0, 2, 2, HALF), F32)
            eq[e0:e1, :, 0:2, :] = jnp.zeros((e1 - e0, 2, 2, HALF), F32)

        @pl.when(k == NK - 1)
        def _():
            ep[e0:e1, :, 66:68, :] = jnp.zeros((e1 - e0, 2, 2, HALF), F32)
            eq[e0:e1, :, 66:68, :] = jnp.zeros((e1 - e0, 2, 2, HALF), F32)

        if g in (0, GROUPS - 1):
            edge = 0 if g == 0 else 18

            @pl.when(b == (0 if g == 0 else NB - 1))
            def _():
                ep[edge:edge + 2] = jnp.zeros((2, 2, Q, HALF), F32)
                eq[edge:edge + 2] = jnp.zeros((2, 2, Q, HALF), F32)

        pl.loop(g * GROUP, (g + 1) * GROUP)(fields_row)
        t5[...] = jnp.dot(f5[...], b5[...], preferred_element_type=F32)
        t9[...] = jnp.dot(f9[...], b9[...], preferred_element_type=F32)
        pl.loop(g * GROUP, (g + 1) * GROUP)(finish_row)
        pick_traces(g)

    for g in range(GROUPS):
        arrive(g)
        if g > 0:
            compute(g - 1)
    compute(GROUPS - 1)

    both = jnp.dot(seg[...], rows[...], preferred_element_type=F32)
    part[...] = both[:, 0:HALF] + both[:, HALF:2 * HALF]

    def part_send(d):
        to = lax.rem(k + d, NK)
        return pltpu.make_async_remote_copy(
            src_ref=part.at[pl.ds(pl.multiple_of(to * F_DEV, F_DEV), F_DEV)], dst_ref=rbuf.at[k],
            send_sem=psend_sem.at[to], recv_sem=precv_sem.at[k],
            device_id=(b, to), device_id_type=MESH)

    def part_recv(d):
        source = lax.rem(k + NK - d, NK)
        return pltpu.make_async_remote_copy(
            src_ref=part.at[0:F_DEV], dst_ref=rbuf.at[source],
            send_sem=psend_sem.at[source], recv_sem=precv_sem.at[source],
            device_id=(b, source), device_id_type=MESH)

    def count_recv(d):
        source = lax.rem(k + NK - d, NK)
        return pltpu.make_async_remote_copy(
            src_ref=cnts.at[0:1], dst_ref=cbuf.at[pl.ds(source, 1)],
            send_sem=csend_sem.at[source], recv_sem=crecv_sem.at[source],
            device_id=(b, source), device_id_type=MESH)

    @pl.loop(1, NK)
    def _(d):
        part_send(d).start()

    def count_sum(d, total):
        count_recv(d).wait_recv()
        return total + cbuf[pl.ds(lax.rem(k + NK - d, NK), 1), :]

    number = lax.fori_loop(1, NK, count_sum, cnts[pl.ds(k, 1), :])
    column = jnp.sum(
        jnp.where(lane[:F_DEV] == sub[:F_DEV], jnp.broadcast_to(number, (F_DEV, HALF)), 0.0),
        axis=1, keepdims=True)

    def part_sum(d, total):
        part_recv(d).wait_recv()
        return total + rbuf[lax.rem(k + NK - d, NK)]

    own_part = part[pl.ds(pl.multiple_of(k * F_DEV, F_DEV), F_DEV), :]
    summed = lax.fori_loop(1, NK, part_sum, own_part)
    prof_out[...] = summed / jnp.maximum(column, 1.0)

    for g in range(GROUPS):
        for dx, dy in peers:
            send(g, peer(dx, dy), lambda copy: copy.wait_send())

        @pl.when(k != NK - 1)
        def _():
            halo_up(g, lambda copy: copy.wait_send())

        @pl.when(k != 0)
        def _():
            halo_down(g, lambda copy: copy.wait_send())

    @pl.loop(1, NK)
    def _(d):
        count_send(d).wait_send()
        part_send(d).wait_send()


def local(amp_traces, patch_owner, patch_fault, patch_trace, patch_offset):
    halves = amp_traces.reshape(NB * CX, 8, 2, HALF).transpose(0, 2, 1, 3)
    table = (PATCHES // HALF, HALF)
    vmem = pl.BlockSpec(memory_space=pltpu.VMEM)
    dma = pltpu.SemaphoreType.DMA
    return pl.pallas_call(
        kernel,
        out_shape=(
            pltpu.VMEM((CX, CY, NT), F32),
            pltpu.VMEM((F_DEV, PATCH), F32),
        ),
        in_specs=[pl.BlockSpec(memory_space=pl.ANY)] * 5,
        out_specs=(vmem, vmem),
        scratch_shapes=[
            pltpu.VMEM(table, jnp.int32),
            pltpu.VMEM(table, jnp.int32),
            pltpu.VMEM(table, jnp.int32),
            pltpu.VMEM(table, jnp.int32),
            pltpu.VMEM((CX + 6, 2, NEAR_C, HALF), F32),
            pltpu.VMEM((CX + 4, 2, Q, HALF), F32),
            pltpu.VMEM((CX + 4, 2, Q, HALF), F32),
            pltpu.VMEM((2, Q, HALF), F32),
            pltpu.VMEM((2, Q, HALF), F32),
            pltpu.VMEM((2, Q, HALF), F32),
            pltpu.VMEM((2, Q, HALF), F32),
            pltpu.VMEM((GROUP * 2 * CY, 2 * NT), BF16),
            pltpu.VMEM((GROUP * 2 * CY, 2 * NT), BF16),
            pltpu.VMEM((GROUP * 2 * CY, NT), F32),
            pltpu.VMEM((GROUP * 2 * CY, NT), F32),
            pltpu.VMEM((2 * NT, NT), BF16),
            pltpu.VMEM((2 * NT, NT), BF16),
            pltpu.VMEM((2 * GROUP * CY, NT), BF16),
            pltpu.VMEM((PATCHES, NT), F32),
            pltpu.VMEM((PATCHES, TRACES), BF16),
            pltpu.VMEM((PATCHES, HALF), jnp.int32),
            pltpu.VMEM((FAULTS, PATCHES), BF16),
            pltpu.VMEM((PATCHES, 2 * HALF), BF16),
            pltpu.VMEM((FAULTS, PATCH), F32),
            pltpu.VMEM((NK, F_DEV, PATCH), F32),
            pltpu.VMEM((NK, HALF), F32),
            pltpu.VMEM((NK, HALF), F32),
            dma((4,)),
            dma((GROUPS,)),
            dma((GROUPS, NB)),
            dma((GROUPS, NB)),
            dma((GROUPS, 2)),
            dma((GROUPS, 2)),
            dma((NK,)),
            dma((NK,)),
            dma((NK,)),
            dma((NK,)),
        ],
        compiler_params=pltpu.CompilerParams(collective_id=0, has_side_effects=True),
        name="fault_attribute",
    )(
        halves,
        patch_owner.reshape(table),
        patch_fault.reshape(table),
        patch_trace.reshape(table),
        patch_offset.reshape(table),
    )


def solution(mesh):
    in_specs = (
        P(None, ("bulk", "brick"), None),
        P(("brick", "bulk"), None),
        P(("brick", "bulk")),
        P(("brick", "bulk")),
        P(("brick", "bulk")),
    )
    out_specs = (P("brick", "bulk", None), P(("brick", "bulk"), None))
    return jax.shard_map(local, mesh=mesh, in_specs=in_specs, out_specs=out_specs, check_vma=False)
```
